512 devices in a mesh: row: 16 (over z_lo, x, core), col: 32 (over z_hi, y).
Axes of the slice: x: 4, y: 8, z: 8 (z_hi: 4, z_lo: 2; z = z_hi * 2 + z_lo), core: 2. Of those that a mesh axis runs over, the one named last changes fastest.
Arguments:
- tiles: bfloat16 [16, 64, 256, 256], P('row', 'col'), may hold values from 0 to 48, as said below
- in_index: int32 [16, 64, 2], P('row', 'col'), may hold values from -1 to 63, as said below
- out_index: int32 [16, 128, 2], P('row', 'col'), may hold values from -1 to 63, as said below
Outputs:
- new_tiles: float32 [16, 128, 256, 256], P('row', 'col')
The draws below stay inside these ranges and needn't reach their ends.
Inputs may be any that keep to these rules, and one draw needn't show every extreme that they name: `tiles`: entries are positive. `in_index`: the device at grid row r and grid column c holds in its 2 slots distinct tiles with block rows r * 4 to (r + 1) * 4 - 1 and block columns c * 2 to (c + 1) * 2 - 1; used slots come first and unused ones hold -1 in both entries. Every diagonal tile (b, b) is stored, and a device that holds diagonal tiles has every slot used. In one grid row and in one grid column every device has every slot used. `out_index`: same layout as in_index with 4 slots: tiles inside the device's region, used slots first, -1 in unused ones, every diagonal tile (b, b) present, every slot used on devices with diagonal tiles and on one whole grid row and one whole grid column.
All inputs are finite; a program needn't handle non-finite values.
Results may differ from the reference program's by a relative error of at most 0.0003.
Values may be sent and summed in bfloat16 or wider, within the bound.
No kernel may reach another device: no remote copies, remote signals or barrier semaphores. Data moves between devices by JAX's collectives and lax.ppermute only.
A program may use at most 64 MiB of HBM per device.

```python
import math
import jax
import jax.numpy as jnp
from jax import lax

TILE = 256
COL_BLOCKS = 2
SLOTS = 2
OUT_SLOTS = 4
NBLK = 64
ROW_BLOCKS = 4
N_ROW = 16
N_COL = 32


def tile_pattern(key, offset_key, slot_count):
    base = jax.random.fold_in(key, offset_key)
    key_list = jax.random.split(base, 5)
    region = ROW_BLOCKS * COL_BLOCKS
    row_level = jax.random.randint(key_list[0], (N_ROW,), 0, 2)
    col_level = jax.random.randint(key_list[1], (N_COL,), 0, 2)
    full_row = jax.random.randint(key_list[2], (), 0, N_ROW)
    full_col = jax.random.randint(key_list[3], (), 0, N_COL)
    row_level = jnp.where(jnp.arange(N_ROW) == full_row, slot_count, row_level)
    col_level = jnp.where(jnp.arange(N_COL) == full_col, slot_count, col_level)
    tile_count = jnp.minimum(slot_count, row_level[:, None] + col_level[None, :])
    grid_rows = jnp.arange(N_ROW)[:, None, None]
    grid_cols = jnp.arange(N_COL)[None, :, None]
    local = jnp.arange(region)[None, None, :]
    block_rows = jnp.broadcast_to(grid_rows * ROW_BLOCKS + local // COL_BLOCKS, (N_ROW, N_COL, region))
    block_cols = jnp.broadcast_to(grid_cols * COL_BLOCKS + local % COL_BLOCKS, (N_ROW, N_COL, region))
    on_diagonal = block_rows == block_cols
    holds_diagonal = jnp.any(on_diagonal, axis=2)
    tile_count = jnp.where(holds_diagonal, slot_count, tile_count)
    priority = jax.random.randint(key_list[4], (N_ROW, N_COL, region), 0, 1 << 20) * region + local
    priority = jnp.where(on_diagonal, priority + (1 << 26), priority)
    _, ranked = lax.top_k(priority, slot_count)
    chosen_rows = jnp.take_along_axis(block_rows, ranked, axis=2)
    chosen_cols = jnp.take_along_axis(block_cols, ranked, axis=2)
    present = jnp.arange(slot_count)[None, None, :] < tile_count[:, :, None]
    chosen_rows = jnp.where(present, chosen_rows, -1)
    chosen_cols = jnp.where(present, chosen_cols, -1)
    paired = jnp.stack([chosen_rows, chosen_cols], axis=-1)
    return paired.reshape(N_ROW, N_COL * slot_count, 2).astype(jnp.int32)


def draw_in_index(key, part):
    return tile_pattern(key, 11, SLOTS)


def draw_out_index(key, part):
    return tile_pattern(key, 23, OUT_SLOTS)


def draw_tiles(key, part):
    paired = tile_pattern(key, 11, SLOTS)
    block_rows = jnp.maximum(paired[..., 0], 0)
    block_cols = jnp.maximum(paired[..., 1], 0)
    row_key = jax.random.fold_in(key, 31)
    col_key = jax.random.fold_in(key, 37)
    value_key = jax.random.fold_in(key, 41)
    node_rows = jnp.exp(jax.random.uniform(row_key, (NBLK, TILE), jnp.float32) * math.log(4.0))
    node_cols = jnp.exp(jax.random.uniform(col_key, (NBLK, TILE), jnp.float32) * math.log(3.0))
    row_scale = jnp.take(node_rows, block_rows, axis=0)
    col_scale = jnp.take(node_cols, block_cols, axis=0)
    uniform_part = jax.random.uniform(value_key, (N_ROW, N_COL * SLOTS, TILE, TILE), jnp.float32)
    position = block_rows.astype(jnp.float32) / (NBLK - 1)
    block_factor = 1.0 + position
    entries = 0.05 + 0.95 * uniform_part
    values = entries * row_scale[..., :, None] * col_scale[..., None, :] * block_factor[..., None, None]
    return values.astype(jnp.bfloat16)


def setup_inputs(seed: int = 0) -> dict:
    streams_of = jax.random.split(jax.random.key(seed), 4)
    tiles = draw_tiles(jax.random.fold_in(streams_of[3], 71), 0)
    in_index = draw_in_index(jax.random.fold_in(streams_of[3], 71), 0)
    out_index = draw_out_index(jax.random.fold_in(streams_of[3], 71), 0)
    return {"tiles": tiles, "in_index": in_index, "out_index": out_index}


def reference(tiles, in_index, out_index):
    flat_tiles = tiles.reshape(-1, TILE, TILE)
    flat_in = in_index.reshape(-1, 2)
    flat_out = out_index.reshape(-1, 2)
    stored = flat_tiles.shape[0]
    present = flat_in[:, 0] >= 0
    safe_rows = jnp.where(present, flat_in[:, 0], NBLK).astype(jnp.int32)
    safe_cols = jnp.where(present, flat_in[:, 1], NBLK).astype(jnp.int32)
    lookup = jnp.full((NBLK + 1, NBLK + 1), -1, jnp.int32)
    lookup = lookup.at[safe_rows, safe_cols].set(jnp.arange(stored, dtype=jnp.int32))
    lookup = lookup[:NBLK, :NBLK]

    def one_tile(pair):
        out_row = pair[0]
        out_col = pair[1]
        used = out_row >= 0
        row_safe = jnp.maximum(out_row, 0)
        col_safe = jnp.maximum(out_col, 0)

        def add_term(running, block):
            left_slot = lookup[row_safe, block]
            right_slot = lookup[block, col_safe]
            both = (left_slot >= 0) & (right_slot >= 0) & used

            def with_term(total):
                left_tile = flat_tiles[jnp.maximum(left_slot, 0)]
                right_tile = flat_tiles[jnp.maximum(right_slot, 0)]
                return total + jnp.dot(left_tile, right_tile, preferred_element_type=jnp.float32)

            def without_term(total):
                return total

            return lax.cond(both, with_term, without_term, running), None

        start_acc = jnp.zeros((TILE, TILE), jnp.float32)
        total, _ = lax.scan(add_term, start_acc, jnp.arange(NBLK, dtype=jnp.int32))
        return total

    expanded = lax.map(one_tile, flat_out)
    squared = expanded * expanded
    out_used = flat_out[:, 0] >= 0
    safe_out_cols = jnp.where(out_used, flat_out[:, 1], NBLK).astype(jnp.int32)
    totals = jnp.zeros((NBLK + 1, TILE), jnp.float32).at[safe_out_cols].add(jnp.sum(squared, axis=1))
    divisor = totals[jnp.where(out_used, flat_out[:, 1], 0).astype(jnp.int32)]
    divisor = jnp.where(out_used[:, None], divisor, 1.0)
    new_tiles = TILE * squared / divisor[:, None, :]
    return new_tiles.reshape(N_ROW, N_COL * OUT_SLOTS, TILE, TILE)
```

```python
import jax
import jax.numpy as jnp
from jax import lax
from jax.experimental import pallas as pl
from jax.experimental.pallas import tpu as pltpu
from jax.sharding import Mesh, PartitionSpec as P

COL_BLOCKS = 2
TILE = 256
PAD = 8
FINE = (("zl", 2), ("x", 4), ("core", 2), ("zh", 4), ("y", 8))
ROW = ("zl", "x", "core")
COL = ("zh", "y")
BUFS = 8


def shift(value, axis, size, by):
    return lax.ppermute(value, axis, [(i, (i + by) % size) for i in range(size)])


def product_kernel(pos_ref, out_ref_index, *refs):
    lefts = refs[:12]
    right, exp_ref, part_ref = refs[12:15]
    todo, lbuf, rbuf, sem = refs[15:]
    counts = [ref.shape[0] for ref in lefts]

    exp_ref[...] = jnp.zeros_like(exp_ref)

    def note(i, n):
        code = pos_ref[i]

        @pl.when(code >= 0)
        def _():
            todo[0, n] = code
            todo[1, n] = i

        return n + (code >= 0).astype(jnp.int32)

    total = lax.fori_loop(0, pos_ref.shape[0], note, jnp.int32(0))

    def start(n):
        slot = n % BUFS
        code = todo[0, n]
        first = 0
        for ref, count in zip(lefts, counts):

            @pl.when((code >= first) & (code < first + count))
            def _(ref=ref, first=first):
                pltpu.make_async_copy(
                    ref.at[code - first, pl.ds(0, TILE)], lbuf.at[slot], sem.at[0, slot]
                ).start()

            first += count
        pltpu.make_async_copy(
            right.at[todo[1, n] % 32, pl.ds(0, TILE)], rbuf.at[slot], sem.at[1, slot]
        ).start()

    def prime(n, carry):
        start(n)
        return carry

    lax.fori_loop(0, jnp.minimum(total, BUFS), prime, 0)

    def multiply(n, carry):
        slot = n % BUFS
        pltpu.make_async_copy(right.at[0, pl.ds(0, TILE)], lbuf.at[slot], sem.at[0, slot]).wait()
        pltpu.make_async_copy(right.at[0, pl.ds(0, TILE)], rbuf.at[slot], sem.at[1, slot]).wait()
        o = todo[1, n] // 32
        exp_ref[o] += jnp.dot(lbuf[slot], rbuf[slot], preferred_element_type=jnp.float32)

        @pl.when(n + BUFS < total)
        def _():
            start(n + BUFS)

        return carry

    lax.fori_loop(0, total, multiply, 0)

    part_ref[...] = jnp.zeros_like(part_ref)
    for o in range(exp_ref.shape[0]):
        value = exp_ref[o]
        squared = value * value
        exp_ref[o] = squared
        column = out_ref_index[o, 1]
        for j in range(COL_BLOCKS):

            @pl.when((column >= 0) & (column % COL_BLOCKS == j))
            def _():
                part_ref[j : j + 1, :] += jnp.sum(squared, axis=0, keepdims=True)


def shards(tiles, in_index, out_index):
    slots = tiles.shape[1]
    out_index = out_index[0]
    out_count = out_index.shape[0]
    marks = jnp.pad(
        in_index[0].astype(tiles.dtype)[:, None, :], ((0, 0), (0, PAD - 1), (0, TILE - 2))
    )
    mine = jnp.concatenate([tiles[0], marks], axis=1)

    pair = jnp.concatenate([mine, shift(mine, "zl", 2, 1)])

    own = lax.all_gather(mine, "y", axis=0, tiled=False)
    right = lax.all_gather(pair, ("x", "core"), axis=0, tiled=True)
    up = shift(mine[0], "zh", 4, 1)
    down = shift(mine[1], "zh", 4, -1)
    early = jnp.stack([up, down, shift(up, "zh", 4, 1), shift(down, "zh", 4, -1)])
    ring = [early]
    ahead = back = early
    for _ in range(3):
        ahead, back = shift(ahead, "y", 8, 1), shift(back, "y", 8, -1)
        ring += [ahead, back]
    ring += [shift(ahead[:2], "y", 8, 1), shift(back[2:], "y", 8, -1)]
    late_up = shift(own[:, 1], "zh", 4, 1)
    late_down = shift(own[:, 0], "zh", 4, -1)
    lefts = [own.reshape(-1, TILE + PAD, TILE)] + ring + [late_up, late_down]

    def index_of(stack):
        return stack[:, TILE, :2].astype(jnp.int32)

    left_index = jnp.concatenate([index_of(stack) for stack in lefts])
    right_index = index_of(right)
    matches = (
        (left_index[None, None, :, 0] == out_index[:, None, None, 0])
        & (left_index[None, None, :, 1] == right_index[None, :, None, 0])
        & (right_index[None, :, None, 1] == out_index[:, None, None, 1])
        & (out_index[:, None, None, 0] >= 0)
    )
    places = jnp.arange(left_index.shape[0], dtype=jnp.int32)
    pos = jnp.max(jnp.where(matches, places, -1), axis=2).reshape(-1)

    squared, part = pl.pallas_call(
        product_kernel,
        grid_spec=pltpu.PrefetchScalarGridSpec(
            num_scalar_prefetch=2,
            grid=(),
            in_specs=[pl.BlockSpec(memory_space=pl.ANY)] * 13,
            out_specs=[pl.BlockSpec(memory_space=pltpu.VMEM)] * 2,
            scratch_shapes=[
                pltpu.SMEM((2, out_count * 32), jnp.int32),
                pltpu.VMEM((BUFS, TILE, TILE), jnp.bfloat16),
                pltpu.VMEM((BUFS, TILE, TILE), jnp.bfloat16),
                pltpu.SemaphoreType.DMA((2, BUFS)),
            ],
        ),
        out_shape=[
            jax.ShapeDtypeStruct((out_count, TILE, TILE), jnp.float32),
            jax.ShapeDtypeStruct((COL_BLOCKS, TILE), jnp.float32),
        ],
    )(pos, out_index, *lefts, right)

    totals = jnp.sum(lax.all_gather(part, ROW, axis=0, tiled=False), axis=0)
    out_used = out_index[:, 0] >= 0
    second = (out_index[:, 1] % COL_BLOCKS == 1)[:, None]
    divisor = jnp.where(second, totals[1][None], totals[0][None])
    divisor = jnp.where(out_used[:, None], divisor, 1.0)
    return (TILE * squared / divisor[:, None, :])[None]


def solution(mesh):
    fine = Mesh(mesh.devices.reshape([size for _, size in FINE]), [name for name, _ in FINE])
    spec = P(ROW, COL)
    return jax.shard_map(
        shards, mesh=fine, in_specs=(spec, spec, spec), out_specs=spec, check_vma=False
    )
```

```python
import jax
import jax.numpy as jnp
from jax import lax
from jax.experimental import pallas as pl
from jax.experimental.pallas import tpu as pltpu
from jax.sharding import Mesh, PartitionSpec as P

COL_BLOCKS = 2
TILE = 256
PAD = 8
FINE = (("zl", 2), ("x", 4), ("core", 2), ("zh", 4), ("y", 8))
ROW = ("zl", "x", "core")
COL = ("zh", "y")
BUFS = 8


def shift(value, axis, size, by):
    return lax.ppermute(value, axis, [(i, (i + by) % size) for i in range(size)])


def product_kernel(pos_ref, out_ref_index, *refs):
    lefts = refs[:12]
    right, exp_ref, part_ref = refs[12:15]
    todo, lbuf, rbuf, sem = refs[15:]
    counts = [ref.shape[0] for ref in lefts]

    exp_ref[...] = jnp.zeros_like(exp_ref)

    def note(i, n):
        code = pos_ref[i]

        @pl.when(code >= 0)
        def _():
            todo[0, n] = code
            todo[1, n] = i

        return n + (code >= 0).astype(jnp.int32)

    total = lax.fori_loop(0, pos_ref.shape[0], note, jnp.int32(0))

    def start(n):
        slot = n % BUFS
        code = todo[0, n]
        first = 0
        for ref, count in zip(lefts, counts):

            @pl.when((code >= first) & (code < first + count))
            def _(ref=ref, first=first):
                pltpu.make_async_copy(
                    ref.at[code - first, pl.ds(0, TILE)], lbuf.at[slot], sem.at[0, slot]
                ).start()

            first += count
        pltpu.make_async_copy(
            right.at[todo[1, n] % 32, pl.ds(0, TILE)], rbuf.at[slot], sem.at[1, slot]
        ).start()

    def prime(n, carry):
        start(n)
        return carry

    lax.fori_loop(0, jnp.minimum(total, BUFS), prime, 0)

    def multiply(n, carry):
        slot = n % BUFS
        pltpu.make_async_copy(right.at[0, pl.ds(0, TILE)], lbuf.at[slot], sem.at[0, slot]).wait()
        pltpu.make_async_copy(right.at[0, pl.ds(0, TILE)], rbuf.at[slot], sem.at[1, slot]).wait()
        o = todo[1, n] // 32
        exp_ref[o] += jnp.dot(lbuf[slot], rbuf[slot], preferred_element_type=jnp.float32)

        @pl.when(n + BUFS < total)
        def _():
            start(n + BUFS)

        return carry

    lax.fori_loop(0, total, multiply, 0)

    part_ref[...] = jnp.zeros_like(part_ref)
    for o in range(exp_ref.shape[0]):
        value = exp_ref[o]
        squared = value * value
        exp_ref[o] = squared
        column = out_ref_index[o, 1]
        for j in range(COL_BLOCKS):

            @pl.when((column >= 0) & (column % COL_BLOCKS == j))
            def _():
                part_ref[j : j + 1, :] += jnp.sum(squared, axis=0, keepdims=True)


def shards(tiles, in_index, out_index):
    slots = tiles.shape[1]
    out_index = out_index[0]
    out_count = out_index.shape[0]
    marks = in_index[0].reshape(1, 1, -1).astype(tiles.dtype)
    marks = jnp.pad(marks, ((0, 0), (0, PAD - 1), (0, TILE - 2 * slots)))
    mine = jnp.concatenate([tiles[0], jnp.broadcast_to(marks, (slots, PAD, TILE))], axis=1)

    own = lax.all_gather(mine, "y", axis=0, tiled=False)
    up = shift(mine[0], "zh", 4, 1)
    down = shift(mine[1], "zh", 4, -1)
    early = jnp.stack([up, down, shift(up, "zh", 4, 1), shift(down, "zh", 4, -1)])
    ring = [early]
    ahead, back = shift(early, "y", 8, 1), shift(early, "y", 8, -1)
    ring += [ahead, back]

    other, _ = lax.optimization_barrier((mine, early))
    other = shift(other, "zl", 2, 1)
    right = lax.all_gather(jnp.concatenate([mine, other]), ("x", "core"), axis=0, tiled=True)

    first, second, ahead, back = lax.optimization_barrier((own[:, 0], own[:, 1], ahead, back))
    late_up = shift(second, "zh", 4, 1)
    late_down = shift(first, "zh", 4, -1)
    for _ in range(2):
        ahead, back = shift(ahead, "y", 8, 1), shift(back, "y", 8, -1)
        ring += [ahead, back]
    ring += [shift(ahead[:2], "y", 8, 1), shift(back[2:], "y", 8, -1)]
    lefts = [own.reshape(-1, TILE + PAD, TILE)] + ring + [late_up, late_down]

    def marks_of(stack):
        return stack[:, TILE, : 2 * slots]

    rows = jnp.concatenate([marks_of(stack) for stack in ring]).reshape(8, 4, 2, 2)
    rows = rows.astype(jnp.int32)
    turn = (lax.axis_index("y") + jnp.array([0, -1, 1, -2, 2, -3, 3, 4], jnp.int32)) % 8
    left_index = jnp.concatenate(
        [
            marks_of(own[:, 0]).astype(jnp.int32).reshape(-1, 2),
            jnp.stack([rows[:, t, t % 2] for t in range(4)], axis=1).reshape(-1, 2),
            rows[:, 0, 1],
            rows[:, 1, 0],
        ]
    )
    places = jnp.concatenate([jnp.arange(48, dtype=jnp.int32), 48 + turn, 56 + turn])
    right_rows = marks_of(right).astype(jnp.int32).reshape(16, 2, 2, 2)
    right_index = jnp.stack([right_rows[:, t, t] for t in range(2)], axis=1).reshape(-1, 2)
    matches = (
        (left_index[None, None, :, 0] == out_index[:, None, None, 0])
        & (left_index[None, None, :, 1] == right_index[None, :, None, 0])
        & (right_index[None, :, None, 1] == out_index[:, None, None, 1])
        & (out_index[:, None, None, 0] >= 0)
    )
    pos = jnp.max(jnp.where(matches, places, -1), axis=2).reshape(-1)

    squared, part = pl.pallas_call(
        product_kernel,
        grid_spec=pltpu.PrefetchScalarGridSpec(
            num_scalar_prefetch=2,
            grid=(),
            in_specs=[pl.BlockSpec(memory_space=pl.ANY)] * 13,
            out_specs=[pl.BlockSpec(memory_space=pltpu.VMEM)] * 2,
            scratch_shapes=[
                pltpu.SMEM((2, out_count * 32), jnp.int32),
                pltpu.VMEM((BUFS, TILE, TILE), jnp.bfloat16),
                pltpu.VMEM((BUFS, TILE, TILE), jnp.bfloat16),
                pltpu.SemaphoreType.DMA((2, BUFS)),
            ],
        ),
        out_shape=[
            jax.ShapeDtypeStruct((out_count, TILE, TILE), jnp.float32),
            jax.ShapeDtypeStruct((COL_BLOCKS, TILE), jnp.float32),
        ],
    )(pos, out_index, *lefts, right)

    parts = jnp.broadcast_to(part[None], (16,) + part.shape)
    totals = jnp.sum(lax.all_to_all(parts, ROW, split_axis=0, concat_axis=0), axis=0)
    out_used = out_index[:, 0] >= 0
    second = (out_index[:, 1] % COL_BLOCKS == 1)[:, None]
    divisor = jnp.where(second, totals[1][None], totals[0][None])
    divisor = jnp.where(out_used[:, None], divisor, 1.0)
    return (TILE * squared / divisor[:, None, :])[None]


def solution(mesh):
    fine = Mesh(mesh.devices.reshape([size for _, size in FINE]), [name for name, _ in FINE])
    spec = P(ROW, COL)
    return jax.shard_map(
        shards, mesh=fine, in_specs=(spec, spec, spec), out_specs=spec, check_vma=False
    )
```

```python
import jax
import jax.numpy as jnp
from jax import lax
from jax.experimental import pallas as pl
from jax.experimental.pallas import tpu as pltpu
from jax.sharding import Mesh, PartitionSpec as P

COL_BLOCKS = 2
TILE = 256
FINE = (("zl", 2), ("x", 4), ("core", 2), ("zh", 4), ("y", 8))
ROW = ("zl", "x", "core")
COL = ("zh", "y")
N_ROW, N_COL, N_ZH, N_Y = 16, 32, 4, 8
RIGHTS = 32
BUFS = 8


def shift(value, axis, size, by):
    return lax.ppermute(value, axis, [(i, (i + by) % size) for i in range(size)])


def to_all(value, axes, size):
    every = jnp.broadcast_to(value[None], (size,) + value.shape)
    return lax.all_to_all(every, axes, split_axis=0, concat_axis=0)


def product_kernel(pos_ref, out_index_ref, *refs):
    lefts = refs[:-7]
    right, exp_ref, part_ref = refs[-7:-4]
    todo, lbuf, rbuf, sem = refs[-4:]

    exp_ref[...] = jnp.zeros_like(exp_ref)

    def note(i, n):
        code = pos_ref[i]

        @pl.when(code >= 0)
        def _():
            todo[0, n] = code
            todo[1, n] = i

        return n + (code >= 0).astype(jnp.int32)

    total = lax.fori_loop(0, pos_ref.shape[0], note, jnp.int32(0))

    def start(n):
        slot = n % BUFS
        code = todo[0, n]
        first = 0
        for ref in lefts:
            count = ref.shape[0]

            @pl.when((code >= first) & (code < first + count))
            def _(ref=ref, first=first):
                pltpu.make_async_copy(ref.at[code - first], lbuf.at[slot], sem.at[0, slot]).start()

            first += count
        pltpu.make_async_copy(
            right.at[todo[1, n] % RIGHTS], rbuf.at[slot], sem.at[1, slot]
        ).start()

    def prime(n, carry):
        start(n)
        return carry

    lax.fori_loop(0, jnp.minimum(total, BUFS), prime, 0)

    def multiply(n, carry):
        slot = n % BUFS
        pltpu.make_async_copy(right.at[0], lbuf.at[slot], sem.at[0, slot]).wait()
        pltpu.make_async_copy(right.at[0], rbuf.at[slot], sem.at[1, slot]).wait()
        o = todo[1, n] // RIGHTS
        exp_ref[o] += jnp.dot(lbuf[slot], rbuf[slot], preferred_element_type=jnp.float32)

        @pl.when(n + BUFS < total)
        def _():
            start(n + BUFS)

        return carry

    lax.fori_loop(0, total, multiply, 0)

    part_ref[...] = jnp.zeros_like(part_ref)
    for o in range(exp_ref.shape[0]):
        value = exp_ref[o]
        squared = value * value
        exp_ref[o] = squared
        column = out_index_ref[o, 1]
        for j in range(COL_BLOCKS):

            @pl.when((column >= 0) & (column % COL_BLOCKS == j))
            def _():
                part_ref[:, j : j + 1, :] += jnp.sum(squared, axis=0, keepdims=True)[None]


def match_table(in_index, out_index):
    row = to_all(in_index.reshape(1, -1), COL, N_COL).reshape(N_ZH, N_Y, -1, 2)
    column = to_all(in_index.reshape(1, -1), ROW, N_ROW).reshape(-1, 2)
    zh, y = lax.axis_index("zh"), lax.axis_index("y")
    hop = (jnp.arange(N_ZH, dtype=jnp.int32)[:, None, None] - zh) % N_ZH
    source = jnp.arange(N_Y, dtype=jnp.int32)[None, :, None]
    slot = jnp.arange(in_index.shape[0], dtype=jnp.int32)[None, None, :]
    away = (source - y) % N_Y
    block = jnp.where(away == 4, 7, jnp.where(away < 4, 2 * away, 2 * (8 - away) - 1))
    place = jnp.where(
        hop == 0,
        2 * source + slot,
        jnp.where(
            hop == 2,
            48 + 2 * block + slot,
            16 + 4 * block + slot + jnp.where(hop == 1, 2, 0),
        ),
    )
    matches = (
        (row[None, None, ..., 0] == out_index[:, 0][:, None, None, None, None])
        & (row[None, None, ..., 1] == column[:, 0][None, :, None, None, None])
        & (column[:, 1][None, :] == out_index[:, 1][:, None])[..., None, None, None]
        & (out_index[:, 0] >= 0)[:, None, None, None, None]
    )
    return jnp.max(jnp.where(matches, place, -1), axis=(2, 3, 4)).reshape(-1)


def shards(tiles, in_index, out_index):
    tiles, in_index, out_index = tiles[0], in_index[0], out_index[0]
    out_count = out_index.shape[0]

    own = lax.all_gather(tiles, "y", axis=0, tiled=True)
    right = lax.all_gather(tiles, ROW, axis=0, tiled=True)
    pos = match_table(in_index, out_index)

    up = shift(tiles, "zh", N_ZH, 1)
    down = shift(tiles, "zh", N_ZH, -1)
    near = [jnp.concatenate([up, down])]
    far = [shift(up, "zh", N_ZH, 1)]

    def step(ring, ahead, back):
        ahead, back = shift(ahead, "y", N_Y, 1), shift(back, "y", N_Y, -1)
        ring += [ahead, back]
        return ahead, back

    near_ends = step(near, near[0], near[0])
    far_ends = step(far, far[0], far[0])
    near_ends, pos = lax.optimization_barrier((near_ends, pos))
    near_ends = step(near, *near_ends)
    far_ends, _ = lax.optimization_barrier((far_ends, near[1:3]))
    far_ends = step(far, *far_ends)
    near_ends, _ = lax.optimization_barrier((near_ends, far[1:3]))
    near_ends = step(near, *near_ends)
    far_ends, _ = lax.optimization_barrier((far_ends, near[3:5]))
    far_ends = step(far, *far_ends)
    near_ends, _ = lax.optimization_barrier((near_ends, far[3:5]))
    near.append(shift(near_ends[1], "y", N_Y, -1))
    far.append(shift(far_ends[0], "y", N_Y, 1))

    lefts = [own] + near + far
    squared, parts = pl.pallas_call(
        product_kernel,
        grid_spec=pltpu.PrefetchScalarGridSpec(
            num_scalar_prefetch=2,
            grid=(),
            in_specs=[pl.BlockSpec(memory_space=pl.ANY)] * (len(lefts) + 1),
            out_specs=[pl.BlockSpec(memory_space=pltpu.VMEM)] * 2,
            scratch_shapes=[
                pltpu.SMEM((2, out_count * RIGHTS), jnp.int32),
                pltpu.VMEM((BUFS, TILE, TILE), jnp.bfloat16),
                pltpu.VMEM((BUFS, TILE, TILE), jnp.bfloat16),
                pltpu.SemaphoreType.DMA((2, BUFS)),
            ],
        ),
        out_shape=[
            jax.ShapeDtypeStruct((out_count, TILE, TILE), jnp.float32),
            jax.ShapeDtypeStruct((N_ROW, COL_BLOCKS, TILE), jnp.float32),
        ],
    )(pos, out_index, *lefts, right)

    totals = jnp.sum(lax.all_to_all(parts, ROW, split_axis=0, concat_axis=0), axis=0)
    out_used = out_index[:, 0] >= 0
    odd = (out_index[:, 1] % COL_BLOCKS == 1)[:, None]
    divisor = jnp.where(odd, totals[1][None], totals[0][None])
    divisor = jnp.where(out_used[:, None], divisor, 1.0)
    return (TILE * squared / divisor[:, None, :])[None]


def solution(mesh):
    fine = Mesh(mesh.devices.reshape([size for _, size in FINE]), [name for name, _ in FINE])
    spec = P(ROW, COL)
    return jax.shard_map(
        shards, mesh=fine, in_specs=(spec, spec, spec), out_specs=spec, check_vma=False
    )
```

```python
import jax
import jax.numpy as jnp
from jax import lax
from jax.experimental import pallas as pl
from jax.experimental.pallas import tpu as pltpu
from jax.sharding import Mesh, PartitionSpec as P

COL_BLOCKS = 2
TILE = 256
FINE = (("zl", 2), ("x", 4), ("core", 2), ("zh", 4), ("y", 8))
ROW = ("zl", "x", "core")
COL = ("zh", "y")
N_ROW, N_ZH, N_Y = 16, 4, 8
RIGHTS = 32
BUFS = 8


def shift(value, axis, size, by):
    return lax.ppermute(value, axis, [(i, (i + by) % size) for i in range(size)])


def to_all(value, axes, size):
    every = jnp.broadcast_to(value[None], (size,) + value.shape)
    return lax.all_to_all(every, axes, split_axis=0, concat_axis=0)


def product_kernel(pos_ref, out_index_ref, *refs):
    lefts = refs[:-7]
    right, exp_ref, part_ref = refs[-7:-4]
    todo, lbuf, rbuf, sem = refs[-4:]

    exp_ref[...] = jnp.zeros_like(exp_ref)

    def note(i, n):
        code = pos_ref[i]

        @pl.when(code >= 0)
        def _():
            todo[0, n] = code
            todo[1, n] = i

        return n + (code >= 0).astype(jnp.int32)

    total = lax.fori_loop(0, pos_ref.shape[0], note, jnp.int32(0))

    def start(n):
        slot = n % BUFS
        code = todo[0, n]
        first = 0
        for ref in lefts:
            count = ref.shape[0]

            @pl.when((code >= first) & (code < first + count))
            def _(ref=ref, first=first):
                pltpu.make_async_copy(ref.at[code - first], lbuf.at[slot], sem.at[0, slot]).start()

            first += count
        pltpu.make_async_copy(
            right.at[todo[1, n] % RIGHTS], rbuf.at[slot], sem.at[1, slot]
        ).start()

    def prime(n, carry):
        start(n)
        return carry

    lax.fori_loop(0, jnp.minimum(total, BUFS), prime, 0)

    def multiply(n, carry):
        slot = n % BUFS
        pltpu.make_async_copy(right.at[0], lbuf.at[slot], sem.at[0, slot]).wait()
        pltpu.make_async_copy(right.at[0], rbuf.at[slot], sem.at[1, slot]).wait()
        o = todo[1, n] // RIGHTS
        exp_ref[o] += jnp.dot(lbuf[slot], rbuf[slot], preferred_element_type=jnp.float32)

        @pl.when(n + BUFS < total)
        def _():
            start(n + BUFS)

        return carry

    lax.fori_loop(0, total, multiply, 0)

    part_ref[...] = jnp.zeros_like(part_ref)
    for o in range(exp_ref.shape[0]):
        value = exp_ref[o]
        squared = value * value
        exp_ref[o] = squared
        column = out_index_ref[o, 1]
        for j in range(COL_BLOCKS):

            @pl.when((column >= 0) & (column % COL_BLOCKS == j))
            def _():
                part_ref[:, j : j + 1, :] += jnp.sum(squared, axis=0, keepdims=True)[None]


def match_table(in_index, out_index):
    row = to_all(to_all(in_index.reshape(1, -1), "zh", N_ZH), "y", N_Y)
    row = row.reshape(N_Y, N_ZH, -1, 2)
    column = to_all(in_index.reshape(1, -1), ROW, N_ROW).reshape(-1, 2)
    source = jnp.arange(N_Y, dtype=jnp.int32)[:, None, None]
    hop = (jnp.arange(N_ZH, dtype=jnp.int32)[None, :, None] - lax.axis_index("zh")) % N_ZH
    slot = jnp.arange(in_index.shape[0], dtype=jnp.int32)[None, None, :]
    away = (source - lax.axis_index("y")) % N_Y
    block = jnp.where(away == 4, 7, jnp.where(away < 4, 2 * away, 2 * (8 - away) - 1))
    kind = jnp.where(hop == 0, 0, jnp.where(hop == 1, 4, 2))
    place = jnp.where(hop == 2, 48 + 2 * source, 6 * block + kind) + slot
    matches = (
        (row[None, None, ..., 0] == out_index[:, 0][:, None, None, None, None])
        & (row[None, None, ..., 1] == column[:, 0][None, :, None, None, None])
        & (column[:, 1][None, :] == out_index[:, 1][:, None])[..., None, None, None]
        & (out_index[:, 0] >= 0)[:, None, None, None, None]
    )
    return jnp.max(jnp.where(matches, place, -1), axis=(2, 3, 4)).reshape(-1)


def shards(tiles, in_index, out_index):
    tiles, in_index, out_index = tiles[0], in_index[0], out_index[0]
    out_count = out_index.shape[0]

    right = lax.all_gather(tiles, ROW, axis=0, tiled=True)
    pos = match_table(in_index, out_index)

    up = shift(tiles, "zh", N_ZH, 1)
    down = shift(tiles, "zh", N_ZH, -1)
    up, down = lax.optimization_barrier((up, down))
    far = shift(up, "zh", N_ZH, 1)
    ahead = back = jnp.concatenate([tiles, up, down])
    ring = [ahead]
    for _ in range(3):
        ahead, back = shift(ahead, "y", N_Y, 1), shift(back, "y", N_Y, -1)
        ring += [ahead, back]
    far, right, _ = lax.optimization_barrier((far, right, ring[1:3]))
    far = lax.all_gather(far, "y", axis=0, tiled=True)
    ahead, back, pos = lax.optimization_barrier((ahead, back, pos))
    ring += [shift(ahead[:3], "y", N_Y, 1), shift(back[3:], "y", N_Y, -1)]

    lefts = ring + [far]
    squared, parts = pl.pallas_call(
        product_kernel,
        grid_spec=pltpu.PrefetchScalarGridSpec(
            num_scalar_prefetch=2,
            grid=(),
            in_specs=[pl.BlockSpec(memory_space=pl.ANY)] * (len(lefts) + 1),
            out_specs=[pl.BlockSpec(memory_space=pltpu.VMEM)] * 2,
            scratch_shapes=[
                pltpu.SMEM((2, out_count * RIGHTS), jnp.int32),
                pltpu.VMEM((BUFS, TILE, TILE), jnp.bfloat16),
                pltpu.VMEM((BUFS, TILE, TILE), jnp.bfloat16),
                pltpu.SemaphoreType.DMA((2, BUFS)),
            ],
        ),
        out_shape=[
            jax.ShapeDtypeStruct((out_count, TILE, TILE), jnp.float32),
            jax.ShapeDtypeStruct((N_ROW, COL_BLOCKS, TILE), jnp.float32),
        ],
    )(pos, out_index, *lefts, right)

    totals = jnp.sum(lax.all_to_all(parts, ROW, split_axis=0, concat_axis=0), axis=0)
    out_used = out_index[:, 0] >= 0
    odd = (out_index[:, 1] % COL_BLOCKS == 1)[:, None]
    divisor = jnp.where(odd, totals[1][None], totals[0][None])
    divisor = jnp.where(out_used[:, None], divisor, 1.0)
    return (TILE * squared / divisor[:, None, :])[None]


def solution(mesh):
    fine = Mesh(mesh.devices.reshape([size for _, size in FINE]), [name for name, _ in FINE])
    spec = P(ROW, COL)
    return jax.shard_map(
        shards, mesh=fine, in_specs=(spec, spec, spec), out_specs=spec, check_vma=False
    )
```

```python
import jax
import jax.numpy as jnp
from jax import lax
from jax.experimental import pallas as pl
from jax.experimental.pallas import tpu as pltpu
from jax.sharding import Mesh, PartitionSpec as P

COL_BLOCKS = 2
TILE = 256
FINE = (("zl", 2), ("x", 4), ("core", 2), ("zh", 4), ("y", 8))
ROW = ("zl", "x", "core")
COL = ("zh", "y")
N_ROW, N_ZH, N_Y = 16, 4, 8
SLOTS = 2
RIGHTS = 32
PAD = 8
PACK = SLOTS * TILE + PAD
BUFS = 8


def shift(value, axis, size, by):
    return lax.ppermute(value, axis, [(i, (i + by) % size) for i in range(size)])


def tile_rows(tile, packed):
    start = tile // SLOTS * PACK + tile % SLOTS * TILE if packed else tile * TILE
    return pl.ds(pl.multiple_of(start, PAD), TILE)


def product_kernel(pos_ref, out_index_ref, *refs):
    lefts = refs[:-7]
    right, exp_ref, part_ref = refs[-7:-4]
    todo, lbuf, rbuf, sem = refs[-4:]

    exp_ref[...] = jnp.zeros_like(exp_ref)

    def note(i, n):
        code = pos_ref[i]

        @pl.when(code >= 0)
        def _():
            todo[0, n] = code
            todo[1, n] = i

        return n + (code >= 0).astype(jnp.int32)

    total = lax.fori_loop(0, pos_ref.shape[0], note, jnp.int32(0))

    def start(n):
        slot = n % BUFS
        code = todo[0, n]
        first = 0
        for ref in lefts:
            rows = ref.shape[0]
            each = rows // PACK * SLOTS if rows % PACK == 0 else rows // TILE

            @pl.when((code >= first) & (code < first + each))
            def _(ref=ref, first=first, rows=rows):
                pltpu.make_async_copy(
                    ref.at[tile_rows(code - first, rows % PACK == 0)], lbuf.at[slot], sem.at[0, slot]
                ).start()

            first += each
        pltpu.make_async_copy(
            right.at[tile_rows(todo[1, n] % RIGHTS, True)], rbuf.at[slot], sem.at[1, slot]
        ).start()

    def prime(n, carry):
        start(n)
        return carry

    lax.fori_loop(0, jnp.minimum(total, BUFS), prime, 0)

    def multiply(n, carry):
        slot = n % BUFS
        pltpu.make_async_copy(right.at[pl.ds(0, TILE)], lbuf.at[slot], sem.at[0, slot]).wait()
        pltpu.make_async_copy(right.at[pl.ds(0, TILE)], rbuf.at[slot], sem.at[1, slot]).wait()
        o = todo[1, n] // RIGHTS
        exp_ref[o] += jnp.dot(lbuf[slot], rbuf[slot], preferred_element_type=jnp.float32)

        @pl.when(n + BUFS < total)
        def _():
            start(n + BUFS)

        return carry

    lax.fori_loop(0, total, multiply, 0)

    part_ref[...] = jnp.zeros_like(part_ref)
    for o in range(exp_ref.shape[0]):
        value = exp_ref[o]
        squared = value * value
        exp_ref[o] = squared
        column = out_index_ref[o, 1]
        for j in range(COL_BLOCKS):

            @pl.when((column >= 0) & (column % COL_BLOCKS == j))
            def _():
                part_ref[:, j : j + 1, :] += jnp.sum(squared, axis=0, keepdims=True)[None]


def match_table(row_index, column_index, out_index):
    matches = (
        (row_index[None, None, :, 0] == out_index[:, None, None, 0])
        & (row_index[None, None, :, 1] == column_index[None, :, None, 0])
        & (column_index[None, :, None, 1] == out_index[:, None, None, 1])
        & (out_index[:, None, None, 0] >= 0)
    )
    places = jnp.arange(row_index.shape[0], dtype=jnp.int32)
    return jnp.max(jnp.where(matches, places, -1), axis=2).reshape(-1)


def shards(tiles, in_index, out_index):
    out_index = out_index[0]
    out_count = out_index.shape[0]
    bare = SLOTS * TILE
    marks = jnp.pad(
        in_index.reshape(1, -1).astype(tiles.dtype), ((0, PAD - 1), (0, TILE - 2 * SLOTS))
    )
    mine = jnp.concatenate([tiles.reshape(bare, TILE), marks])

    right = lax.all_gather(mine, ROW, axis=0, tiled=True)

    up = shift(mine, "zh", N_ZH, 1)
    down = shift(mine, "zh", N_ZH, -1)
    up, down = lax.optimization_barrier((up, down))
    far = shift(up, "zh", N_ZH, 1)
    packs = (mine, up, down)
    signs = [pack[bare : bare + 1] for pack in packs]
    signs.append(jnp.zeros((PAD - len(packs), TILE), tiles.dtype))
    ahead = back = jnp.concatenate([pack[:bare] for pack in packs] + signs)
    ring = [ahead]
    for turn in range(3):
        if turn == 2:
            ahead, back, right = lax.optimization_barrier((ahead, back, right))
        ahead, back = shift(ahead, "y", N_Y, 1), shift(back, "y", N_Y, -1)
        ring += [ahead, back]
    far, _ = lax.optimization_barrier((far, ring[1:3]))
    far = lax.all_gather(far, "y", axis=0, tiled=True)
    half = 3 * TILE
    last = [shift(ahead[:half], "y", N_Y, 1), shift(back[half:], "y", N_Y, -1)]
    far, last = lax.optimization_barrier((far, last))

    def signs_of(stack, first, count):
        return stack[first : first + count, : 2 * SLOTS]

    row_signs = [signs_of(block, 2 * half, 3) for block in ring] + [signs_of(last[1], half, 3)]
    row_signs.append(signs_of(far.reshape(N_Y, PACK, TILE)[:, bare], 0, N_Y))
    row_index = jnp.concatenate(row_signs).astype(jnp.int32).reshape(-1, 2)
    column_index = signs_of(right.reshape(N_ROW, PACK, TILE)[:, bare], 0, N_ROW)
    pos = match_table(row_index, column_index.astype(jnp.int32).reshape(-1, 2), out_index)

    lefts = ring + last + [far]
    squared, parts = pl.pallas_call(
        product_kernel,
        grid_spec=pltpu.PrefetchScalarGridSpec(
            num_scalar_prefetch=2,
            grid=(),
            in_specs=[pl.BlockSpec(memory_space=pl.ANY)] * (len(lefts) + 1),
            out_specs=[pl.BlockSpec(memory_space=pltpu.VMEM)] * 2,
            scratch_shapes=[
                pltpu.SMEM((2, out_count * RIGHTS), jnp.int32),
                pltpu.VMEM((BUFS, TILE, TILE), jnp.bfloat16),
                pltpu.VMEM((BUFS, TILE, TILE), jnp.bfloat16),
                pltpu.SemaphoreType.DMA((2, BUFS)),
            ],
        ),
        out_shape=[
            jax.ShapeDtypeStruct((out_count, TILE, TILE), jnp.float32),
            jax.ShapeDtypeStruct((N_ROW, COL_BLOCKS, TILE), jnp.float32),
        ],
    )(pos, out_index, *lefts, right)

    totals = jnp.sum(lax.all_to_all(parts, ROW, split_axis=0, concat_axis=0), axis=0)
    out_used = out_index[:, 0] >= 0
    odd = (out_index[:, 1] % COL_BLOCKS == 1)[:, None]
    divisor = jnp.where(odd, totals[1][None], totals[0][None])
    divisor = jnp.where(out_used[:, None], divisor, 1.0)
    return (TILE * squared / divisor[:, None, :])[None]


def solution(mesh):
    fine = Mesh(mesh.devices.reshape([size for _, size in FINE]), [name for name, _ in FINE])
    spec = P(ROW, COL)
    return jax.shard_map(
        shards, mesh=fine, in_specs=(spec, spec, spec), out_specs=spec, check_vma=False
    )
```

```python
import jax
import jax.numpy as jnp
from jax import lax
from jax.experimental import pallas as pl
from jax.experimental.pallas import tpu as pltpu
from jax.sharding import Mesh, PartitionSpec as P

COL_BLOCKS = 2
TILE = 256
PAD = 8
FINE = (("zl", 2), ("x", 4), ("core", 2), ("zh", 4), ("y", 8))
ROW = ("zl", "x", "core")
COL = ("zh", "y")
BUFS = 8


def shift(value, axis, size, by):
    return lax.ppermute(value, axis, [(i, (i + by) % size) for i in range(size)])


def product_kernel(pos_ref, out_ref_index, *refs):
    lefts = refs[:12]
    right, exp_ref, part_ref = refs[12:15]
    todo, lbuf, rbuf, sem = refs[15:]
    counts = [ref.shape[0] for ref in lefts]

    exp_ref[...] = jnp.zeros_like(exp_ref)

    def note(i, n):
        code = pos_ref[i]

        @pl.when(code >= 0)
        def _():
            todo[0, n] = code
            todo[1, n] = i

        return n + (code >= 0).astype(jnp.int32)

    total = lax.fori_loop(0, pos_ref.shape[0], note, jnp.int32(0))

    def start(n):
        slot = n % BUFS
        code = todo[0, n]
        first = 0
        for ref, count in zip(lefts, counts):

            @pl.when((code >= first) & (code < first + count))
            def _(ref=ref, first=first):
                pltpu.make_async_copy(
                    ref.at[code - first, pl.ds(0, TILE)], lbuf.at[slot], sem.at[0, slot]
                ).start()

            first += count
        pltpu.make_async_copy(
            right.at[todo[1, n] % 32, pl.ds(0, TILE)], rbuf.at[slot], sem.at[1, slot]
        ).start()

    def prime(n, carry):
        start(n)
        return carry

    lax.fori_loop(0, jnp.minimum(total, BUFS), prime, 0)

    def multiply(n, carry):
        slot = n % BUFS
        pltpu.make_async_copy(right.at[0, pl.ds(0, TILE)], lbuf.at[slot], sem.at[0, slot]).wait()
        pltpu.make_async_copy(right.at[0, pl.ds(0, TILE)], rbuf.at[slot], sem.at[1, slot]).wait()
        o = todo[1, n] // 32
        exp_ref[o] += jnp.dot(lbuf[slot], rbuf[slot], preferred_element_type=jnp.float32)

        @pl.when(n + BUFS < total)
        def _():
            start(n + BUFS)

        return carry

    lax.fori_loop(0, total, multiply, 0)

    part_ref[...] = jnp.zeros_like(part_ref)
    for o in range(exp_ref.shape[0]):
        value = exp_ref[o]
        squared = value * value
        exp_ref[o] = squared
        column = out_ref_index[o, 1]
        for j in range(COL_BLOCKS):

            @pl.when((column >= 0) & (column % COL_BLOCKS == j))
            def _():
                part_ref[:, j : j + 1, :] += jnp.sum(squared, axis=0, keepdims=True)[None]


def shards(tiles, in_index, out_index):
    slots = tiles.shape[1]
    out_index = out_index[0]
    out_count = out_index.shape[0]
    marks = jnp.pad(
        in_index[0].astype(tiles.dtype)[:, None, :], ((0, 0), (0, PAD - 1), (0, TILE - 2))
    )
    mine = jnp.concatenate([tiles[0], marks], axis=1)

    own = lax.all_gather(mine, "y", axis=0, tiled=False)
    up = shift(mine[0], "zh", 4, 1)
    down = shift(mine[1], "zh", 4, -1)
    other = shift(mine, "zl", 2, 1)
    up, down, other = lax.optimization_barrier((up, down, other))
    early = jnp.stack([up, down, shift(up, "zh", 4, 1), shift(down, "zh", 4, -1)])
    other, _ = lax.optimization_barrier((other, early))
    right = lax.all_gather(jnp.concatenate([mine, other]), ("x", "core"), axis=0, tiled=True)
    ring = [early]
    ahead = back = early
    for turn in range(3):
        if turn == 1:
            first, second, ahead, back = lax.optimization_barrier(
                (own[:, 0], own[:, 1], ahead, back)
            )
            late_up = shift(second, "zh", 4, 1)
            late_down = shift(first, "zh", 4, -1)
        ahead, back = shift(ahead, "y", 8, 1), shift(back, "y", 8, -1)
        ring += [ahead, back]
    ring += [shift(ahead[:2], "y", 8, 1), shift(back[2:], "y", 8, -1)]
    lefts = [own.reshape(-1, TILE + PAD, TILE)] + ring + [late_up, late_down]

    def index_of(stack):
        return stack[:, TILE, :2].astype(jnp.int32)

    left_index = jnp.concatenate([index_of(stack) for stack in lefts])
    right_index = index_of(right)
    matches = (
        (left_index[None, None, :, 0] == out_index[:, None, None, 0])
        & (left_index[None, None, :, 1] == right_index[None, :, None, 0])
        & (right_index[None, :, None, 1] == out_index[:, None, None, 1])
        & (out_index[:, None, None, 0] >= 0)
    )
    places = jnp.arange(left_index.shape[0], dtype=jnp.int32)
    pos = jnp.max(jnp.where(matches, places, -1), axis=2).reshape(-1)

    squared, parts = pl.pallas_call(
        product_kernel,
        grid_spec=pltpu.PrefetchScalarGridSpec(
            num_scalar_prefetch=2,
            grid=(),
            in_specs=[pl.BlockSpec(memory_space=pl.ANY)] * 13,
            out_specs=[pl.BlockSpec(memory_space=pltpu.VMEM)] * 2,
            scratch_shapes=[
                pltpu.SMEM((2, out_count * 32), jnp.int32),
                pltpu.VMEM((BUFS, TILE, TILE), jnp.bfloat16),
                pltpu.VMEM((BUFS, TILE, TILE), jnp.bfloat16),
                pltpu.SemaphoreType.DMA((2, BUFS)),
            ],
        ),
        out_shape=[
            jax.ShapeDtypeStruct((out_count, TILE, TILE), jnp.float32),
            jax.ShapeDtypeStruct((16, COL_BLOCKS, TILE), jnp.float32),
        ],
    )(pos, out_index, *lefts, right)

    totals = jnp.sum(lax.all_to_all(parts, ROW, split_axis=0, concat_axis=0), axis=0)
    out_used = out_index[:, 0] >= 0
    second = (out_index[:, 1] % COL_BLOCKS == 1)[:, None]
    divisor = jnp.where(second, totals[1][None], totals[0][None])
    divisor = jnp.where(out_used[:, None], divisor, 1.0)
    return (TILE * squared / divisor[:, None, :])[None]


def solution(mesh):
    fine = Mesh(mesh.devices.reshape([size for _, size in FINE]), [name for name, _ in FINE])
    spec = P(ROW, COL)
    return jax.shard_map(
        shards, mesh=fine, in_specs=(spec, spec, spec), out_specs=spec, check_vma=False
    )
```

```python
import jax
import jax.numpy as jnp
from jax import lax
from jax.experimental import pallas as pl
from jax.experimental.pallas import tpu as pltpu
from jax.sharding import Mesh, PartitionSpec as P

COL_BLOCKS = 2
SLOTS = 2
TILE = 256
LATE = 192
PART = TILE - LATE
PAD = 8
PACK = SLOTS * TILE + PAD
FINE = (("zl", 2), ("x", 4), ("core", 2), ("zh", 4), ("y", 8))
ROW = ("zl", "x", "core")
COL = ("zh", "y")
UP, DOWN, UP2, DOWN2, MARKS = 0, TILE + PART, 2 * (TILE + PART), 3 * TILE + 2 * PART, 4 * TILE + 2 * PART
TURNS = (0, -1, 1, -2, 2, -3, 3, 4)
N_Y = len(TURNS)
OWN_TILES = N_Y * SLOTS
RING_TILES = 4 * N_Y
RIGHTS = 32
BUFS = 8


def shift(value, axis, size, by):
    return lax.ppermute(value, axis, [(i, (i + by) % size) for i in range(size)])


def rows_at(start, count):
    return pl.ds(pl.multiple_of(start, PAD), count)


def convert_kernel(in_ref, out_ref):
    out_ref[...] = in_ref[...].astype(jnp.int32)


def product_kernel(pos_ref, out_ref_index, source_ref, *refs):
    own, ring, (late_up, late_down) = refs[0], refs[1 : 1 + N_Y], refs[1 + N_Y : 3 + N_Y]
    right, exp_ref, part_ref, todo, lbuf, rbuf, sem = refs[3 + N_Y :]

    exp_ref[...] = jnp.zeros_like(exp_ref)

    def note(i, n):
        code = pos_ref[i]

        @pl.when(code >= 0)
        def _():
            todo[0, n] = code
            todo[1, n] = i

        return n + (code >= 0).astype(jnp.int32)

    total = lax.fori_loop(0, pos_ref.shape[0], note, jnp.int32(0))

    def pack_rows(tile):
        return rows_at(tile // SLOTS * PACK + tile % SLOTS * TILE, TILE)

    def start(n):
        slot = n % BUFS
        code = todo[0, n]

        def from_block(block, offset, count, target):
            for j, ref in enumerate(ring):

                @pl.when(block == j)
                def _(ref=ref):
                    rows = ref.at[rows_at(offset, count)]
                    pltpu.make_async_copy(rows, target, sem.at[0, slot]).start()

        @pl.when(code < OWN_TILES)
        def _():
            pltpu.make_async_copy(own.at[pack_rows(code)], lbuf.at[slot], sem.at[0, slot]).start()

        @pl.when((code >= OWN_TILES) & (code < OWN_TILES + RING_TILES))
        def _():
            kind = code % 4
            offset = jnp.where(
                kind < 2, jnp.where(kind == 0, UP, DOWN), jnp.where(kind == 2, UP2, DOWN2)
            )
            from_block((code - OWN_TILES) // 4, offset, TILE, lbuf.at[slot])

        for late, offset, first in (
            (late_up, UP + TILE, OWN_TILES + RING_TILES),
            (late_down, DOWN + TILE, OWN_TILES + RING_TILES + N_Y),
        ):

            @pl.when((code >= first) & (code < first + N_Y))
            def _(late=late, offset=offset, first=first):
                block = code - first
                pltpu.make_async_copy(
                    late.at[source_ref[block], pl.ds(0, LATE)],
                    lbuf.at[slot, pl.ds(0, LATE)],
                    sem.at[0, slot],
                ).start()
                from_block(block, offset, PART, lbuf.at[slot, pl.ds(LATE, PART)])

        pltpu.make_async_copy(
            right.at[pack_rows(todo[1, n] % RIGHTS)], rbuf.at[slot], sem.at[1, slot]
        ).start()

    def prime(n, carry):
        start(n)
        return carry

    lax.fori_loop(0, jnp.minimum(total, BUFS), prime, 0)

    def multiply(n, carry):
        slot = n % BUFS
        pltpu.make_async_copy(right.at[pl.ds(0, TILE)], lbuf.at[slot], sem.at[0, slot]).wait()
        pltpu.make_async_copy(right.at[pl.ds(0, TILE)], rbuf.at[slot], sem.at[1, slot]).wait()
        o = todo[1, n] // RIGHTS
        exp_ref[o] += jnp.dot(lbuf[slot], rbuf[slot], preferred_element_type=jnp.float32)

        @pl.when(n + BUFS < total)
        def _():
            start(n + BUFS)

        return carry

    lax.fori_loop(0, total, multiply, 0)

    part_ref[...] = jnp.zeros_like(part_ref)
    for o in range(exp_ref.shape[0]):
        value = exp_ref[o]
        squared = value * value
        exp_ref[o] = squared
        column = out_ref_index[o, 1]
        for j in range(COL_BLOCKS):

            @pl.when((column >= 0) & (column % COL_BLOCKS == j))
            def _():
                part_ref[:, j : j + 1, :] += jnp.sum(squared, axis=0, keepdims=True)[None]


def shards(tiles, in_index, out_index):
    tiles, out_index = tiles[0], out_index[0]
    out_count = out_index.shape[0]
    marks = jnp.pad(
        in_index.reshape(1, -1).astype(tiles.dtype), ((0, PAD - 1), (0, TILE - 2 * SLOTS))
    )
    mine = jnp.concatenate([tiles[0], tiles[1], marks])

    own = lax.all_gather(mine, "y", axis=0, tiled=False)
    other = shift(mine, "zl", 2, 1)
    up = shift(jnp.concatenate([tiles[0], tiles[1, LATE:], marks]), "zh", 4, 1)
    down = shift(jnp.concatenate([tiles[1], tiles[0, LATE:], marks]), "zh", 4, -1)
    up2 = shift(jnp.concatenate([tiles[0], marks]), "zh", 4, 2)
    down2 = shift(jnp.concatenate([tiles[1], marks]), "zh", 4, -2)
    hops = (up, down, up2, down2)
    signs = [hop[-PAD : 1 - PAD] for hop in hops] + [jnp.zeros((PAD - 4, TILE), tiles.dtype)]
    early = jnp.concatenate([hop[:-PAD] for hop in hops] + signs)
    other, early = lax.optimization_barrier((other, early))
    right = lax.all_gather(jnp.concatenate([mine, other]), ("x", "core"), axis=0, tiled=True)

    ring = [early]
    ahead = back = early
    for turn in range(3):
        if turn == 1:
            first, second, ahead, back = lax.optimization_barrier(
                (
                    jnp.concatenate([own[:, :LATE], own[:, -PAD:]], axis=1),
                    jnp.concatenate([own[:, TILE : TILE + LATE], own[:, -PAD:]], axis=1),
                    ahead,
                    back,
                )
            )
            late_up = shift(second, "zh", 4, 1)
            late_down = shift(first, "zh", 4, -1)
        ahead, back = shift(ahead, "y", N_Y, 1), shift(back, "y", N_Y, -1)
        ring += [ahead, back]
    ring.append(shift(back, "y", N_Y, -1))
    lefts = [own.reshape(-1, TILE)] + ring + [late_up, late_down]

    def signs_of(stack):
        return stack[..., : 2 * SLOTS]

    rows = [signs_of(block[MARKS : MARKS + 4]) for block in ring]
    rows = jnp.concatenate(rows).astype(jnp.int32).reshape(N_Y, 4, SLOTS, 2)
    late_rows = pl.pallas_call(
        convert_kernel,
        out_shape=jax.ShapeDtypeStruct((2 * N_Y, TILE), jnp.int32),
        cost_estimate=pl.CostEstimate(flops=2_000_000_000, bytes_accessed=0, transcendentals=0),
    )(jnp.concatenate([late_up[:, LATE], late_down[:, LATE]]))
    left_index = jnp.concatenate(
        [
            signs_of(own[:, -PAD]).astype(jnp.int32).reshape(-1, 2),
            jnp.stack([rows[:, t, t % 2] for t in range(4)], axis=1).reshape(-1, 2),
            late_rows[:N_Y, 2:4],
            late_rows[N_Y:, :2],
        ]
    )
    me = lax.axis_index("y")
    away = (jnp.arange(N_Y, dtype=jnp.int32) - me) % N_Y
    block = jnp.where(away == 4, 7, jnp.where(away < 4, 2 * away, 2 * (N_Y - away) - 1))
    fixed = OWN_TILES + RING_TILES
    places = jnp.concatenate(
        [jnp.arange(fixed, dtype=jnp.int32), fixed + block, fixed + N_Y + block]
    )
    sources = (me + jnp.array(TURNS, jnp.int32)) % N_Y
    right_index = signs_of(right.reshape(-1, PACK, TILE)[:, -PAD]).astype(jnp.int32).reshape(-1, 2)
    matches = (
        (left_index[None, None, :, 0] == out_index[:, None, None, 0])
        & (left_index[None, None, :, 1] == right_index[None, :, None, 0])
        & (right_index[None, :, None, 1] == out_index[:, None, None, 1])
        & (out_index[:, None, None, 0] >= 0)
    )
    pos = jnp.max(jnp.where(matches, places, -1), axis=2).reshape(-1)

    squared, parts = pl.pallas_call(
        product_kernel,
        grid_spec=pltpu.PrefetchScalarGridSpec(
            num_scalar_prefetch=3,
            grid=(),
            in_specs=[pl.BlockSpec(memory_space=pl.ANY)] * (len(lefts) + 1),
            out_specs=[pl.BlockSpec(memory_space=pltpu.VMEM)] * 2,
            scratch_shapes=[
                pltpu.SMEM((2, out_count * RIGHTS), jnp.int32),
                pltpu.VMEM((BUFS, TILE, TILE), jnp.bfloat16),
                pltpu.VMEM((BUFS, TILE, TILE), jnp.bfloat16),
                pltpu.SemaphoreType.DMA((2, BUFS)),
            ],
        ),
        out_shape=[
            pltpu.VMEM((out_count, TILE, TILE), jnp.float32),
            pltpu.VMEM((16, COL_BLOCKS, TILE), jnp.float32),
        ],
    )(pos, out_index, sources, *lefts, right)

    totals = jnp.sum(lax.all_to_all(parts, ROW, split_axis=0, concat_axis=0), axis=0)
    out_used = out_index[:, 0] >= 0
    second = (out_index[:, 1] % COL_BLOCKS == 1)[:, None]
    divisor = jnp.where(second, totals[1][None], totals[0][None])
    divisor = jnp.where(out_used[:, None], divisor, 1.0)
    return (TILE * squared / divisor[:, None, :])[None]


def solution(mesh):
    fine = Mesh(mesh.devices.reshape([size for _, size in FINE]), [name for name, _ in FINE])
    spec = P(ROW, COL)
    return jax.shard_map(
        shards, mesh=fine, in_specs=(spec, spec, spec), out_specs=spec, check_vma=False
    )
```

```python
import jax
import jax.numpy as jnp
from jax import lax
from jax.experimental import pallas as pl
from jax.experimental.pallas import tpu as pltpu
from jax.sharding import Mesh, PartitionSpec as P

COL_BLOCKS = 2
SLOTS = 2
TILE = 256
LATE = 192
PART = TILE - LATE
PAD = 8
PACK = SLOTS * TILE + PAD
FINE = (("zl", 2), ("x", 4), ("core", 2), ("zh", 4), ("y", 8))
ROW = ("zl", "x", "core")
COL = ("zh", "y")
UP, DOWN, UP2, DOWN2, MARKS = 0, TILE + PART, 2 * (TILE + PART), 3 * TILE + 2 * PART, 4 * TILE + 2 * PART
TURNS = (0, -1, 1, -2, 2, -3, 3, 4)
N_Y = len(TURNS)
OWN_TILES = N_Y * SLOTS
RING_TILES = 4 * N_Y
RIGHTS = 32
BUFS = 8


def shift(value, axis, size, by):
    return lax.ppermute(value, axis, [(i, (i + by) % size) for i in range(size)])


def rows_at(start, count):
    return pl.ds(pl.multiple_of(start, PAD), count)


def convert_kernel(in_ref, out_ref):
    out_ref[...] = in_ref[...].astype(jnp.int32)


def product_kernel(pos_ref, out_ref_index, source_ref, *refs):
    own, ring, (late_up, late_down) = refs[0], refs[1 : 1 + N_Y], refs[1 + N_Y : 3 + N_Y]
    right, exp_ref, part_ref, todo, lbuf, rbuf, sem = refs[3 + N_Y :]

    def note(i, n):
        code = pos_ref[i]

        todo[0, n] = code
        todo[1, n] = i
        return n + (code >= 0).astype(jnp.int32)

    total = lax.fori_loop(0, pos_ref.shape[0], note, jnp.int32(0))

    def pack_rows(tile):
        return rows_at(tile // SLOTS * PACK + tile % SLOTS * TILE, TILE)

    def start(n):
        slot = n % BUFS
        code = todo[0, n]

        def from_block(block, offset, count, target):
            for j, ref in enumerate(ring):

                @pl.when(block == j)
                def _(ref=ref):
                    rows = ref.at[rows_at(offset, count)]
                    pltpu.make_async_copy(rows, target, sem.at[0, slot]).start()

        @pl.when(code < OWN_TILES)
        def _():
            pltpu.make_async_copy(own.at[pack_rows(code)], lbuf.at[slot], sem.at[0, slot]).start()

        @pl.when((code >= OWN_TILES) & (code < OWN_TILES + RING_TILES))
        def _():
            kind = code % 4
            offset = jnp.where(
                kind < 2, jnp.where(kind == 0, UP, DOWN), jnp.where(kind == 2, UP2, DOWN2)
            )
            from_block((code - OWN_TILES) // 4, offset, TILE, lbuf.at[slot])

        for late, offset, first in (
            (late_up, UP + TILE, OWN_TILES + RING_TILES),
            (late_down, DOWN + TILE, OWN_TILES + RING_TILES + N_Y),
        ):

            @pl.when((code >= first) & (code < first + N_Y))
            def _(late=late, offset=offset, first=first):
                block = code - first
                pltpu.make_async_copy(
                    late.at[source_ref[block], pl.ds(0, LATE)],
                    lbuf.at[slot, pl.ds(0, LATE)],
                    sem.at[0, slot],
                ).start()
                from_block(block, offset, PART, lbuf.at[slot, pl.ds(LATE, PART)])

        pltpu.make_async_copy(
            right.at[pack_rows(todo[1, n] % RIGHTS)], rbuf.at[slot], sem.at[1, slot]
        ).start()

    def prime(n, carry):
        start(n)
        return carry

    lax.fori_loop(0, jnp.minimum(total, BUFS), prime, 0)
    exp_ref[...] = jnp.zeros_like(exp_ref)

    def multiply(n, carry):
        slot = n % BUFS
        pltpu.make_async_copy(right.at[pl.ds(0, TILE)], lbuf.at[slot], sem.at[0, slot]).wait()
        pltpu.make_async_copy(right.at[pl.ds(0, TILE)], rbuf.at[slot], sem.at[1, slot]).wait()
        o = todo[1, n] // RIGHTS
        exp_ref[o] += jnp.dot(lbuf[slot], rbuf[slot], preferred_element_type=jnp.float32)

        @pl.when(n + BUFS < total)
        def _():
            start(n + BUFS)

        return carry

    lax.fori_loop(0, total, multiply, 0)

    part_ref[...] = jnp.zeros_like(part_ref)
    for o in range(exp_ref.shape[0]):
        value = exp_ref[o]
        squared = value * value
        exp_ref[o] = squared
        column = out_ref_index[o, 1]
        for j in range(COL_BLOCKS):

            @pl.when((column >= 0) & (column % COL_BLOCKS == j))
            def _():
                part_ref[:, j : j + 1, :] += jnp.sum(squared, axis=0, keepdims=True)[None]


def shards(tiles, in_index, out_index):
    tiles, out_index = tiles[0], out_index[0]
    out_count = out_index.shape[0]
    marks = jnp.pad(
        in_index.reshape(1, -1).astype(tiles.dtype), ((0, PAD - 1), (0, TILE - 2 * SLOTS))
    )
    mine = jnp.concatenate([tiles[0], tiles[1], marks])

    own = lax.all_gather(mine, "y", axis=0, tiled=False)
    other = shift(mine, "zl", 2, 1)
    up = shift(jnp.concatenate([tiles[0], tiles[1, LATE:], marks]), "zh", 4, 1)
    down = shift(jnp.concatenate([tiles[1], tiles[0, LATE:], marks]), "zh", 4, -1)
    up2 = shift(jnp.concatenate([tiles[0], marks]), "zh", 4, 2)
    down2 = shift(jnp.concatenate([tiles[1], marks]), "zh", 4, -2)
    hops = (up, down, up2, down2)
    signs = [hop[-PAD : 1 - PAD] for hop in hops] + [jnp.zeros((PAD - 4, TILE), tiles.dtype)]
    early = jnp.concatenate([hop[:-PAD] for hop in hops] + signs)
    other, early = lax.optimization_barrier((other, early))
    right = lax.all_gather(jnp.concatenate([mine, other]), ("x", "core"), axis=0, tiled=True)

    ring = [early]
    ahead = back = early
    for turn in range(3):
        if turn == 1:
            first, second, ahead, back = lax.optimization_barrier(
                (
                    jnp.concatenate([own[:, :LATE], own[:, -PAD:]], axis=1),
                    jnp.concatenate([own[:, TILE : TILE + LATE], own[:, -PAD:]], axis=1),
                    ahead,
                    back,
                )
            )
            late_up = shift(second, "zh", 4, 1)
            late_down = shift(first, "zh", 4, -1)
        ahead, back = shift(ahead, "y", N_Y, 1), shift(back, "y", N_Y, -1)
        ring += [ahead, back]
    ring.append(shift(back, "y", N_Y, -1))
    lefts = [own.reshape(-1, TILE)] + ring + [late_up, late_down]

    def signs_of(stack):
        return stack[..., : 2 * SLOTS]

    rows = [signs_of(block[MARKS : MARKS + 4]) for block in ring]
    rows = jnp.concatenate(rows).astype(jnp.int32).reshape(N_Y, 4, SLOTS, 2)
    late_rows = pl.pallas_call(
        convert_kernel,
        out_shape=jax.ShapeDtypeStruct((2 * N_Y, TILE), jnp.int32),
        cost_estimate=pl.CostEstimate(flops=2_000_000_000, bytes_accessed=0, transcendentals=0),
    )(jnp.concatenate([late_up[:, LATE], late_down[:, LATE]]))
    left_index = jnp.concatenate(
        [
            signs_of(own[:, -PAD]).astype(jnp.int32).reshape(-1, 2),
            jnp.stack([rows[:, t, t % 2] for t in range(4)], axis=1).reshape(-1, 2),
            late_rows[:N_Y, 2:4],
            late_rows[N_Y:, :2],
        ]
    )
    me = lax.axis_index("y")
    away = (jnp.arange(N_Y, dtype=jnp.int32) - me) % N_Y
    block = jnp.where(away == 4, 7, jnp.where(away < 4, 2 * away, 2 * (N_Y - away) - 1))
    fixed = OWN_TILES + RING_TILES
    places = jnp.concatenate(
        [jnp.arange(fixed, dtype=jnp.int32), fixed + block, fixed + N_Y + block]
    )
    sources = (me + jnp.array(TURNS, jnp.int32)) % N_Y
    right_index = signs_of(right.reshape(-1, PACK, TILE)[:, -PAD]).astype(jnp.int32).reshape(-1, 2)
    matches = (
        (left_index[None, None, :, 0] == out_index[:, None, None, 0])
        & (left_index[None, None, :, 1] == right_index[None, :, None, 0])
        & (right_index[None, :, None, 1] == out_index[:, None, None, 1])
        & (out_index[:, None, None, 0] >= 0)
    )
    pos = jnp.max(jnp.where(matches, places, -1), axis=2).reshape(-1)

    squared, parts = pl.pallas_call(
        product_kernel,
        grid_spec=pltpu.PrefetchScalarGridSpec(
            num_scalar_prefetch=3,
            grid=(),
            in_specs=[pl.BlockSpec(memory_space=pl.ANY)] * (len(lefts) + 1),
            out_specs=[pl.BlockSpec(memory_space=pltpu.VMEM)] * 2,
            scratch_shapes=[
                pltpu.SMEM((2, out_count * RIGHTS), jnp.int32),
                pltpu.VMEM((BUFS, TILE, TILE), jnp.bfloat16),
                pltpu.VMEM((BUFS, TILE, TILE), jnp.bfloat16),
                pltpu.SemaphoreType.DMA((2, BUFS)),
            ],
        ),
        out_shape=[
            pltpu.VMEM((out_count, TILE, TILE), jnp.float32),
            pltpu.VMEM((16, COL_BLOCKS, TILE), jnp.float32),
        ],
    )(pos, out_index, sources, *lefts, right)

    totals = jnp.sum(lax.all_to_all(parts, ROW, split_axis=0, concat_axis=0), axis=0)
    out_used = out_index[:, 0] >= 0
    second = (out_index[:, 1] % COL_BLOCKS == 1)[:, None]
    divisor = jnp.where(second, totals[1][None], totals[0][None])
    divisor = jnp.where(out_used[:, None], divisor, 1.0)
    return (TILE * squared / divisor[:, None, :])[None]


def solution(mesh):
    fine = Mesh(mesh.devices.reshape([size for _, size in FINE]), [name for name, _ in FINE])
    spec = P(ROW, COL)
    return jax.shard_map(
        shards, mesh=fine, in_specs=(spec, spec, spec), out_specs=spec, check_vma=False
    )
```
